32 devices in a mesh: groups: 2 (over x), dom: 16 (over z, y, core).
Axes of the slice: x: 2, y: 2, z: 4, core: 2. Of those that a mesh axis runs over, the one named last changes fastest.
Arguments:
- features: bfloat16 [4, 32768, 256], P('groups', 'dom'), parts along dimension 0, may hold values from -6 to 6
- cotangent: bfloat16 [4, 32768, 256], P('groups', 'dom'), parts along dimension 0, may hold values from -6 to 6
- adjacency: bfloat16 [256, 4, 128, 128], P('dom'), may hold values from -0.25 to 0.25
- tile_cols: int32 [256, 4], P('dom'), may hold values from 0 to 255, as said below
- tile_counts: int32 [256], P('dom'), may hold values from 1 to 4, as said below
- w_self: bfloat16 [256, 256], replicated, may hold values from -0.375 to 0.375
- w_neigh: bfloat16 [256, 256], replicated, may hold values from -0.375 to 0.375
- w_out: bfloat16 [256, 256], replicated, may hold values from -0.375 to 0.375
Outputs:
- updated: bfloat16 [4, 32768, 256], P('groups', 'dom'), parts along dimension 0
- grad_features: bfloat16 [4, 32768, 256], P('groups', 'dom'), parts along dimension 0
- grad_self: float32 [512, 256], P('groups'), parts along dimension 0
- grad_neigh: float32 [512, 256], P('groups'), parts along dimension 0
- grad_out: float32 [512, 256], P('groups'), parts along dimension 0
The draws below stay inside these ranges and needn't reach their ends.
There are 2 independent parts, one for each index of `groups`. The reference program is written for one: setup_inputs(seed, part) draws one part's arguments, and reference() takes and returns one part's arrays. A program takes and returns all parts, laid end to end along the dimension named above; an argument that names none is the same for every part. Nothing has to cross between parts.
Inputs may be any that keep to these rules, and one draw needn't show every extreme that they name: tile_cols[r, k] - r lies between -4 and 4 (both reached); block rows of even index have tile_cols[r, 0] = min(r + 4, 255), odd ones max(r - 4, 0); a block column may repeat in a row. `tile_counts`: block rows whose index is a multiple of 3 have 4 live slots.
All inputs are finite; a program needn't handle non-finite values.
Results may differ from the reference program's by a relative error of at most 0.0054.
Values may be sent and summed in bfloat16 or wider, within the bound.
No kernel may reach another device: no remote copies, remote signals or barrier semaphores. Data moves between devices by JAX's collectives and lax.ppermute only.
A program may use at most 128 MiB of HBM per device.

```python
import math
import jax
import jax.numpy as jnp
from jax import lax

F = 256
BLK = 128
KT = 4
R = 4
CLONES = 2
BPD = 16
NB = 256
NODES = 32768


def draw_tile_cols(key, part):
    row_ids = jnp.arange(NB, dtype=jnp.int32)
    first_slot = jnp.where(row_ids % 2 == 0, R, -R).astype(jnp.int32)
    others = jax.random.randint(jax.random.fold_in(key, 11), (NB, KT - 1), -R, R + 1, dtype=jnp.int32)
    offsets = jnp.concatenate([first_slot[:, None], others], axis=1)
    return jnp.clip(row_ids[:, None] + offsets, 0, NB - 1).astype(jnp.int32)


def draw_tile_counts(key, part):
    row_ids = jnp.arange(NB, dtype=jnp.int32)
    random_counts = jax.random.randint(jax.random.fold_in(key, 23), (NB,), 1, KT + 1, dtype=jnp.int32)
    return jnp.where(row_ids % 3 == 0, KT, random_counts).astype(jnp.int32)


def level_of(own_key, extent, split, low, largest):
    level = 1.0
    for position, parts in split:
        heights = jax.random.uniform(jax.random.fold_in(jax.random.fold_in(own_key, 6), position), (parts,), jnp.float32, low / len(split), largest / len(split))
        level = level * jnp.repeat(jnp.exp(heights), extent[position] // parts).reshape((-1,) + (1,) * (len(extent) - 1 - position))
    return level


def normal_values(key, dims, scale, most, shards=(), kind=jnp.bfloat16):
    result = scale * jax.random.normal(key, dims, jnp.float32)
    if shards:
        result = result * level_of(key, dims, shards, -0.22, 0.18)
    return jnp.clip(result, -most, most).astype(kind)


def setup_inputs(seed: int = 0, part: int = 0) -> dict:
    key_list = jax.random.split(jax.random.key(seed), 9)
    own_keys = jax.random.split(jax.random.fold_in(key_list[8], part), 9)
    return {
        "features": normal_values(own_keys[0], (CLONES, NODES, F), 1.0, 6.0, ((1, 16),)),
        "cotangent": normal_values(own_keys[1], (CLONES, NODES, F), 1.0, 6.0, ((1, 16),)),
        "adjacency": normal_values(key_list[2], (NB, KT, BLK, BLK), (BLK * KT) ** -0.5, 0.25, ((0, 16),)),
        "tile_cols": draw_tile_cols(jax.random.fold_in(key_list[8], 71), part),
        "tile_counts": draw_tile_counts(jax.random.fold_in(key_list[8], 71), part),
        "w_self": normal_values(key_list[5], (F, F), F ** -0.5, 0.375),
        "w_neigh": normal_values(key_list[6], (F, F), F ** -0.5, 0.375),
        "w_out": normal_values(key_list[7], (F, F), F ** -0.5, 0.375),
    }


def reference(features, cotangent, adjacency, tile_cols, tile_counts, w_self, w_neigh, w_out):
    slot_ids = jnp.arange(KT, dtype=jnp.int32)
    live_mask = slot_ids[None, :] < tile_counts[:, None]
    live_tiles = jnp.where(live_mask[:, :, None, None], adjacency, jnp.zeros((), jnp.bfloat16))
    state_blocks = features.reshape(CLONES, NB, BLK, F)

    def aggregate_row(row_block):
        picked = jnp.take(state_blocks, tile_cols[row_block], axis=1)
        return jnp.einsum('kij,ckjf->cif', live_tiles[row_block].astype(jnp.float32), picked.astype(jnp.float32))
    gathered = lax.map(aggregate_row, jnp.arange(NB, dtype=jnp.int32))
    aggregate = gathered.transpose(1, 0, 2, 3).reshape(CLONES * NODES, F).astype(jnp.bfloat16)
    flat_state = features.reshape(CLONES * NODES, F)
    pre = jnp.dot(flat_state, w_self, preferred_element_type=jnp.float32) + jnp.dot(aggregate, w_neigh, preferred_element_type=jnp.float32)
    sigma = jax.nn.sigmoid(pre)
    activated = (pre * sigma).astype(jnp.bfloat16)
    updated = (flat_state.astype(jnp.float32) + jnp.dot(activated, w_out, preferred_element_type=jnp.float32)).astype(jnp.bfloat16)
    flat_cot = cotangent.reshape(CLONES * NODES, F)
    grad_act = jnp.dot(flat_cot, w_out.T, preferred_element_type=jnp.float32)
    d_pre = (grad_act * sigma * (1.0 + pre * (1.0 - sigma))).astype(jnp.bfloat16)
    factor = 1.0 / math.sqrt(2.0 * NODES)
    grad_out = jnp.dot(activated.T, flat_cot, preferred_element_type=jnp.float32) * factor
    grad_self = jnp.dot(flat_state.T, d_pre, preferred_element_type=jnp.float32) * factor
    grad_neigh = jnp.dot(aggregate.T, d_pre, preferred_element_type=jnp.float32) * factor
    d_aggregate = jnp.dot(d_pre, w_neigh.T, preferred_element_type=jnp.float32).astype(jnp.bfloat16).reshape(CLONES, NB, BLK, F)
    direct = flat_cot.astype(jnp.float32) + jnp.dot(d_pre, w_self.T, preferred_element_type=jnp.float32)

    def scatter_row(carry, row_block):
        own_total, lower_total, upper_total = carry
        cols = tile_cols[row_block]
        row_group = row_block // BPD
        col_group = cols // BPD
        same_mask = (col_group == row_group).astype(jnp.float32)[None, :, None, None]
        lower_mask = (col_group > row_group).astype(jnp.float32)[None, :, None, None]
        upper_mask = (col_group < row_group).astype(jnp.float32)[None, :, None, None]
        contrib = jnp.einsum('kij,cif->ckjf', live_tiles[row_block].astype(jnp.float32), d_aggregate[:, row_block].astype(jnp.float32))
        own_total = own_total.at[:, cols].add(contrib * same_mask)
        lower_total = lower_total.at[:, cols].add(contrib * lower_mask)
        upper_total = upper_total.at[:, cols].add(contrib * upper_mask)
        return ((own_total, lower_total, upper_total), None)
    start_total = jnp.zeros((CLONES, NB, BLK, F), jnp.float32)
    totals, unused = lax.scan(scatter_row, (start_total, start_total, start_total), jnp.arange(NB, dtype=jnp.int32))
    own_total, lower_total, upper_total = totals
    from_lower = lax.optimization_barrier(lower_total.astype(jnp.bfloat16)).astype(jnp.float32)
    from_upper = lax.optimization_barrier(upper_total.astype(jnp.bfloat16)).astype(jnp.float32)
    transposed = own_total + from_lower + from_upper
    grad_features = (direct + transposed.reshape(CLONES * NODES, F)).astype(jnp.bfloat16)
    return (updated.reshape(CLONES, NODES, F), grad_features.reshape(CLONES, NODES, F), grad_self, grad_neigh, grad_out)
```

```python
import functools
import math

import jax
import jax.numpy as jnp
from jax import lax
from jax.experimental import pallas as pl
from jax.experimental.pallas import tpu as pltpu
from jax.sharding import PartitionSpec as P

R = 4
F32 = jnp.float32
BF16 = jnp.bfloat16
ANY = pl.BlockSpec(memory_space=pl.ANY)
VM = pl.BlockSpec(memory_space=pltpu.VMEM)
SM = pl.BlockSpec(memory_space=pltpu.SMEM)
PARAMS = pltpu.CompilerParams(vmem_limit_bytes=56 * 1024 * 1024)


def mm(a, b):
    return lax.dot_general(a, b, (((1,), (0,)), ((), ())), preferred_element_type=F32)


def mm_bt(a, b):
    return lax.dot_general(a, b, (((1,), (1,)), ((), ())), preferred_element_type=F32)


def mm_at(a, b):
    return lax.dot_general(a, b, (((0,), (0,)), ((), ())), preferred_element_type=F32)


def block_at(index, size):
    return pl.ds(pl.multiple_of(index * size, size), size)


def start_all(copies):
    for copy in copies:
        copy.start()
    return copies


def wait_all(copies):
    for copy in copies:
        copy.wait()


def load_row(a_ref, row, live, slots):
    return jnp.concatenate(
        [jnp.where(k < live, a_ref[row, k], jnp.zeros((), BF16)) for k in range(slots)], axis=1
    )


def aggregate_rows(a_ref, acat_ref, agg_ref, x_ref, cols, live, slots, size):
    clones = x_ref.shape[0]
    for r in range(R):
        acat = load_row(a_ref, r, live(r), slots)
        acat_ref[r] = acat
        for c in range(clones):
            picked = jnp.concatenate(
                [x_ref[c, block_at(cols(r, k), size), :] for k in range(slots)], axis=0
            )
            agg_ref[c, r * size : (r + 1) * size, :] = mm(acat, picked).astype(BF16)


def dense_forward(x, agg, cot, ws, wn, wo):
    pre = mm(x, ws) + mm(agg, wn)
    sigma = jax.nn.sigmoid(pre)
    act = (pre * sigma).astype(BF16)
    d_pre = (mm_bt(cot, wo) * sigma * (1.0 + pre * (1.0 - sigma))).astype(BF16)
    return act, d_pre


def main_kernel(
    idx, cols_ref, cnt_ref, x_hbm, nh_hbm, a_hbm, cot_hbm, ws, wn, wo,
    upd_hbm, acc_hbm, nmsg_hbm, g_hbm,
    xe, a_s, cot_s, acc, upd_s, nmsg_s, g_s, acat_s, agg_s, da_s, sems,
):
    clones, rows, hidden = x_hbm.shape
    per, slots, size, _ = a_hbm.shape
    width = R * size
    chunks = per // R - 1
    odd = lax.rem(idx[0], 2)
    first = idx[0] * per - R
    off = jnp.where(odd == 1, 0, R)
    near = jnp.where(odd == 1, 0, R + per)
    ins = start_all(
        [
            pltpu.make_async_copy(x_hbm, xe.at[:, pl.ds(width, rows), :], sems.at[0]),
            pltpu.make_async_copy(
                nh_hbm, xe.at[:, pl.ds(pl.multiple_of(near * size, width), width), :], sems.at[1]
            ),
        ]
    )
    a_in, cot_in = [], []
    for i in range(chunks):
        a_in += start_all(
            [pltpu.make_async_copy(a_hbm.at[pl.ds(off + R * i, R)], a_s.at[i], sems.at[2 + i])]
        )
        start = pl.multiple_of((off + R * i) * size, width)
        cot_in += start_all(
            [
                pltpu.make_async_copy(
                    cot_hbm.at[:, pl.ds(start, width), :], cot_s.at[i], sems.at[2 + chunks + i]
                )
            ]
        )
    acc[...] = jnp.zeros_like(acc)
    outs = []
    wait_all(ins)
    for i in range(chunks):
        a_in[i].wait()
        base = off + R * i
        start = pl.multiple_of(base * size, width)

        def cols(r, k):
            return cols_ref[base + r, k] - first

        aggregate_rows(
            a_s.at[i], acat_s, agg_s, xe, cols, lambda r: cnt_ref[base + r], slots, size
        )
        cot_in[i].wait()
        for c in range(clones):
            x = xe[c, pl.ds(start + width, width), :]
            agg = agg_s[c]
            cot = cot_s[i, c]
            act, d_pre = dense_forward(x, agg, cot, ws[...], wn[...], wo[...])
            upd_s[i, c] = (x.astype(F32) + mm(act, wo[...])).astype(BF16)
            parts = (mm_at(x, d_pre), mm_at(agg, d_pre), mm_at(act, cot))
            for p, part in enumerate(parts):
                sl = slice(p * hidden, (p + 1) * hidden)
                if i == 0 and c == 0:
                    g_s[sl, :] = part
                else:
                    g_s[sl, :] += part
            da_s[:, c * hidden : (c + 1) * hidden] = mm_bt(d_pre, wn[...]).astype(BF16)
            acc[c, pl.ds(start + width, width), :] += cot.astype(F32) + mm_bt(d_pre, ws[...])
        outs += start_all(
            [
                pltpu.make_async_copy(
                    upd_s.at[i], upd_hbm.at[:, pl.ds(start, width), :], sems.at[2 + 2 * chunks + i]
                )
            ]
        )
        for r in range(R):
            msg = mm_at(acat_s[r], da_s[r * size : (r + 1) * size, :])
            for k in range(slots):
                for c in range(clones):
                    at = block_at(cols(r, k), size)
                    acc[c, at, :] += msg[k * size : (k + 1) * size, c * hidden : (c + 1) * hidden]
    nmsg_s[...] = acc[:, pl.ds(pl.multiple_of(near * size, width), width), :].astype(BF16)
    last = 2 + 3 * chunks
    outs += start_all(
        [
            pltpu.make_async_copy(nmsg_s, nmsg_hbm, sems.at[last]),
            pltpu.make_async_copy(g_s, g_hbm, sems.at[last + 1]),
            pltpu.make_async_copy(acc.at[:, pl.ds(width, rows), :], acc_hbm, sems.at[last + 2]),
        ]
    )
    wait_all(outs)


def far_kernel(
    idx, cols_ref, cnt_ref, x_hbm, fh_hbm, a_hbm, cot_hbm, g_hbm, ws, wn, wo,
    fmsg_ref, keep_ref, send_ref, act_ref, dpre_ref, da_ref,
    xw, a_s, cot_s, g_s, fm_s, acat_s, agg_s, sems,
):
    clones, rows, hidden = x_hbm.shape
    per, slots, size, _ = a_hbm.shape
    width = R * size
    odd = lax.rem(idx[0], 2)
    first = idx[0] * per
    base = jnp.where(odd == 1, per - R, 0)
    start = pl.multiple_of(base * size, width)
    window = first + jnp.where(odd == 1, per - 2 * R, -R)
    halo_at = pl.multiple_of(jnp.where(odd == 1, 2 * width, 0), width)
    local_at = pl.multiple_of(jnp.where(odd == 1, 0, width), width)
    local_from = pl.multiple_of(jnp.where(odd == 1, rows - 2 * width, 0), width)
    ins = start_all(
        [
            pltpu.make_async_copy(fh_hbm, xw.at[:, pl.ds(halo_at, width), :], sems.at[0]),
            pltpu.make_async_copy(
                x_hbm.at[:, pl.ds(local_from, 2 * width), :],
                xw.at[:, pl.ds(local_at, 2 * width), :],
                sems.at[1],
            ),
            pltpu.make_async_copy(a_hbm.at[pl.ds(base, R)], a_s, sems.at[2]),
            pltpu.make_async_copy(cot_hbm.at[:, pl.ds(start, width), :], cot_s, sems.at[3]),
            pltpu.make_async_copy(g_hbm, g_s, sems.at[4]),
        ]
    )
    fm_s[...] = jnp.zeros_like(fm_s)
    wait_all(ins)

    def cols(r, k):
        return cols_ref[base + r, k] - window

    aggregate_rows(a_s, acat_s, agg_s, xw, cols, lambda r: cnt_ref[base + r], slots, size)
    mine = pl.multiple_of(jnp.where(odd == 1, width, width), width)
    for c in range(clones):
        x = xw[c, pl.ds(mine, width), :]
        agg = agg_s[c]
        cot = cot_s[c]
        act, d_pre = dense_forward(x, agg, cot, ws[...], wn[...], wo[...])
        act_ref[c] = act
        dpre_ref[c] = d_pre
        da_ref[:, c * hidden : (c + 1) * hidden] = mm_bt(d_pre, wn[...]).astype(BF16)
        parts = (mm_at(x, d_pre), mm_at(agg, d_pre), mm_at(act, cot))
        for p, part in enumerate(parts):
            g_s[p * hidden : (p + 1) * hidden, :] += part
    halo_block = jnp.where(odd == 1, 2 * R, 0)
    for r in range(R):
        for k in range(slots):
            target = cols(r, k) - halo_block

            @pl.when((k < cnt_ref[base + r]) & (target >= 0) & (target < R))
            def _():
                msg = mm_at(a_s[r, k], da_ref[r * size : (r + 1) * size, :])
                for c in range(clones):
                    fm_s[c, block_at(target, size), :] += msg[:, c * hidden : (c + 1) * hidden]

    fmsg_ref[...] = fm_s[...].astype(BF16)
    half = g_s.shape[0] // 2
    keep_ref[...] = g_s[pl.ds(pl.multiple_of(odd * half, half), half), :]
    send_ref[...] = g_s[pl.ds(pl.multiple_of((1 - odd) * half, half), half), :]


def last_kernel(
    idx, cols_ref, cnt_ref, x_hbm, a_hbm, cot_hbm, acc_hbm, nrecv_hbm, frecv_hbm, act_hbm, dpre_hbm, da_hbm,
    ws, wo, upd_in, upd_hbm, grad_hbm,
    acc, a_s, x_s, cot_s, near_s, far_s, act_s, dpre_s, da_s, upd_s, grad_s, sems,
):
    clones, rows, hidden = x_hbm.shape
    per, slots, size, _ = a_hbm.shape
    width = R * size
    odd = lax.rem(idx[0], 2)
    first = idx[0] * per
    base = jnp.where(odd == 1, per - R, 0)
    start = pl.multiple_of(base * size, width)
    near_start = pl.multiple_of(jnp.where(odd == 1, 0, rows - width), width)
    pairs = (
        (a_hbm.at[pl.ds(base, R)], a_s),
        (x_hbm.at[:, pl.ds(start, width), :], x_s),
        (cot_hbm.at[:, pl.ds(start, width), :], cot_s),
        (act_hbm, act_s),
        (dpre_hbm, dpre_s),
        (da_hbm, da_s),
        (acc_hbm, acc),
        (nrecv_hbm, near_s),
        (frecv_hbm, far_s),
    )
    ins = start_all([pltpu.make_async_copy(s, d, sems.at[j]) for j, (s, d) in enumerate(pairs)])
    wait_all(ins)
    for c in range(clones):
        upd_s[c] = (x_s[c].astype(F32) + mm(act_s[c], wo[...])).astype(BF16)
    store = pltpu.make_async_copy(upd_s, upd_hbm.at[:, pl.ds(start, width), :], sems.at[len(pairs)])
    store.start()
    for c in range(clones):
        acc[c, pl.ds(start, width), :] += (
            cot_s[c].astype(F32) + mm_bt(dpre_s[c], ws[...]) + far_s[c].astype(F32)
        )
        acc[c, pl.ds(near_start, width), :] += near_s[c].astype(F32)
    for r in range(R):
        for k in range(slots):
            target = cols_ref[base + r, k] - first

            @pl.when((k < cnt_ref[base + r]) & (target >= 0) & (target < per))
            def _():
                msg = mm_at(a_s[r, k], da_s[r * size : (r + 1) * size, :])
                for c in range(clones):
                    acc[c, block_at(target, size), :] += msg[:, c * hidden : (c + 1) * hidden]

    grad_s[...] = acc[...].astype(BF16)
    out = pltpu.make_async_copy(grad_s, grad_hbm, sems.at[len(pairs) + 1])
    out.start()
    store.wait()
    out.wait()


def swap(value, bit):
    count = lax.axis_size("dom")
    return lax.ppermute(value, "dom", [(i, i ^ bit) for i in range(count)])


def halves(value, high):
    half = value.shape[0] // 2
    low_part, high_part = value[:half], value[half:]
    return jnp.where(high, high_part, low_part), jnp.where(high, low_part, high_part)


def join(mine, other, high):
    return jnp.where(
        high, jnp.concatenate([other, mine], axis=0), jnp.concatenate([mine, other], axis=0)
    )


def reduce_all(keep, send, index, factor):
    count = lax.axis_size("dom")
    total = keep + swap(send, 1)
    bits = [1 << b for b in range(1, count.bit_length() - 1)]
    scatter = bits[-2:] if len(bits) > 2 else []
    for bit in scatter:
        mine, other = halves(total, (index & bit) != 0)
        total = mine + swap(other.astype(BF16), bit).astype(F32)
    for bit in bits:
        if bit not in scatter:
            rounded = total.astype(BF16)
            total = rounded.astype(F32) + swap(rounded, bit).astype(F32)
    result = total.astype(BF16)
    for bit in reversed(scatter):
        result = join(result, swap(result, bit), (index & bit) != 0)
    result = join(result, swap(result, 1), (index & 1) != 0)
    return result.astype(F32) * factor


def body(features, cotangent, adjacency, tile_cols, tile_counts, w_self, w_neigh, w_out):
    clones, rows, hidden = features.shape
    per, slots, size, _ = adjacency.shape
    width = R * size
    count = lax.axis_size("dom")
    index = lax.axis_index("dom")
    odd = (index & 1) == 1
    idx = index.reshape(1).astype(jnp.int32)
    near_pairs = [(i, i ^ 1) for i in range(count)]
    far_pairs = [(i, ((i + 1) ^ 1) - 1) for i in range(1, count - 1)]
    far_start = jnp.where(odd, rows - width, 0)
    near_start = jnp.where(odd, 0, rows - width)
    far_out = lax.dynamic_slice_in_dim(features, far_start, width, axis=1)
    near_out = lax.dynamic_slice_in_dim(features, near_start, width, axis=1)
    far_halo = lax.ppermute(far_out, "dom", far_pairs)
    near_halo = lax.ppermute(near_out, "dom", near_pairs)

    sds = jax.ShapeDtypeStruct
    chunks = per // R - 1
    upd, acc, near_msg, g = pl.pallas_call(
        main_kernel,
        out_shape=(
            sds((clones, rows, hidden), BF16),
            sds((clones, rows, hidden), F32),
            sds((clones, width, hidden), BF16),
            sds((3 * hidden, hidden), F32),
        ),
        in_specs=[SM, SM, SM, ANY, ANY, ANY, ANY, VM, VM, VM],
        out_specs=(ANY, ANY, ANY, ANY),
        scratch_shapes=[
            pltpu.VMEM((clones, rows + 2 * width, hidden), BF16),
            pltpu.VMEM((chunks, R, slots, size, size), BF16),
            pltpu.VMEM((chunks, clones, width, hidden), BF16),
            pltpu.VMEM((clones, rows + 2 * width, hidden), F32),
            pltpu.VMEM((chunks, clones, width, hidden), BF16),
            pltpu.VMEM((clones, width, hidden), BF16),
            pltpu.VMEM((3 * hidden, hidden), F32),
            pltpu.VMEM((R, size, slots * size), BF16),
            pltpu.VMEM((clones, width, hidden), BF16),
            pltpu.VMEM((width, clones * hidden), BF16),
            pltpu.SemaphoreType.DMA((5 + 3 * chunks,)),
        ],
        compiler_params=PARAMS,
        name="near_rows",
    )(idx, tile_cols, tile_counts, features, near_halo, adjacency, cotangent, w_self, w_neigh, w_out)
    near_recv = lax.ppermute(near_msg, "dom", near_pairs)

    far_msg, keep, send, act, d_pre, d_agg = pl.pallas_call(
        far_kernel,
        out_shape=(
            sds((clones, width, hidden), BF16),
            sds((3 * hidden // 2, hidden), F32),
            sds((3 * hidden // 2, hidden), F32),
            sds((clones, width, hidden), BF16),
            sds((clones, width, hidden), BF16),
            sds((width, clones * hidden), BF16),
        ),
        in_specs=[SM, SM, SM, ANY, ANY, ANY, ANY, ANY, VM, VM, VM],
        out_specs=(VM,) * 6,
        scratch_shapes=[
            pltpu.VMEM((clones, 3 * width, hidden), BF16),
            pltpu.VMEM((R, slots, size, size), BF16),
            pltpu.VMEM((clones, width, hidden), BF16),
            pltpu.VMEM((3 * hidden, hidden), F32),
            pltpu.VMEM((clones, width, hidden), F32),
            pltpu.VMEM((R, size, slots * size), BF16),
            pltpu.VMEM((clones, width, hidden), BF16),
            pltpu.SemaphoreType.DMA((5,)),
        ],
        compiler_params=PARAMS,
        name="far_rows",
    )(idx, tile_cols, tile_counts, features, far_halo, adjacency, cotangent, g, w_self, w_neigh, w_out)
    far_recv = lax.ppermute(far_msg, "dom", far_pairs)

    factor = 1.0 / math.sqrt(2.0 * rows * count)
    sums = reduce_all(keep, send, index, factor)

    updated, grad_features = pl.pallas_call(
        last_kernel,
        out_shape=(sds((clones, rows, hidden), BF16), sds((clones, rows, hidden), BF16)),
        in_specs=[SM, SM, SM] + [ANY] * 9 + [VM, VM, ANY],
        out_specs=(ANY, ANY),
        input_output_aliases={14: 0},
        scratch_shapes=[
            pltpu.VMEM((clones, rows, hidden), F32),
            pltpu.VMEM((R, slots, size, size), BF16),
            pltpu.VMEM((clones, width, hidden), BF16),
            pltpu.VMEM((clones, width, hidden), BF16),
            pltpu.VMEM((clones, width, hidden), BF16),
            pltpu.VMEM((clones, width, hidden), BF16),
            pltpu.VMEM((clones, width, hidden), BF16),
            pltpu.VMEM((clones, width, hidden), BF16),
            pltpu.VMEM((width, clones * hidden), BF16),
            pltpu.VMEM((clones, width, hidden), BF16),
            pltpu.VMEM((clones, rows, hidden), BF16),
            pltpu.SemaphoreType.DMA((11,)),
        ],
        compiler_params=PARAMS,
        name="last_rows",
    )(
        idx, tile_cols, tile_counts, features, adjacency, cotangent, acc, near_recv, far_recv,
        act, d_pre, d_agg, w_self, w_out, upd,
    )
    return (
        updated,
        grad_features,
        sums[:hidden],
        sums[hidden : 2 * hidden],
        sums[2 * hidden :],
    )


def solution(mesh):
    return jax.shard_map(
        body,
        mesh=mesh,
        in_specs=(
            P("groups", "dom", None),
            P("groups", "dom", None),
            P("dom", None, None, None),
            P("dom", None),
            P("dom"),
            P(),
            P(),
            P(),
        ),
        out_specs=(
            P("groups", "dom", None),
            P("groups", "dom", None),
            P("groups", None),
            P("groups", None),
            P("groups", None),
        ),
        check_vma=False,
    )
```

```python
import functools
import math

import jax
import jax.numpy as jnp
from jax import lax
from jax.experimental import pallas as pl
from jax.experimental.pallas import tpu as pltpu
from jax.sharding import PartitionSpec as P

R = 4
F32 = jnp.float32
BF16 = jnp.bfloat16
ANY = pl.BlockSpec(memory_space=pltpu.HBM)
VM = pl.BlockSpec(memory_space=pltpu.VMEM)
SM = pl.BlockSpec(memory_space=pltpu.SMEM)
OWN_AT, EDGE_AT = 2, 3
COSTS = dict(mid_rows=1, near_rows=1, far_rows=1, messages=1, own_rows=1, edge_rows=1)
LIMIT = 12 * 1024 * 1024


def mm(a, b):
    return lax.dot_general(a, b, (((1,), (0,)), ((), ())), preferred_element_type=F32)


def mm_bt(a, b):
    return lax.dot_general(a, b, (((1,), (1,)), ((), ())), preferred_element_type=F32)


def mm_at(a, b):
    return lax.dot_general(a, b, (((0,), (0,)), ((), ())), preferred_element_type=F32)


def block_at(index, size):
    return pl.ds(pl.multiple_of(index * size, size), size)


def start_all(copies):
    for copy in copies:
        copy.start()
    return copies


def wait_all(copies):
    for copy in copies:
        copy.wait()


def in_vmem(value):
    return pltpu.with_memory_space_constraint(value, pltpu.VMEM)


def in_hbm(value):
    return pltpu.with_memory_space_constraint(value, pltpu.HBM)


def aggregate_rows(a_ref, acat_ref, agg_ref, x_ref, cols, live):
    slots, size = a_ref.shape[1:3]
    for r in range(R):
        acat = jnp.concatenate(
            [jnp.where(k < live(r), a_ref[r, k], jnp.zeros((), BF16)) for k in range(slots)], axis=1
        )
        acat_ref[r] = acat
        for c in range(x_ref.shape[0]):
            picked = jnp.concatenate(
                [x_ref[c, block_at(cols(r, k), size), :] for k in range(slots)], axis=0
            )
            agg_ref[c, r * size : (r + 1) * size, :] = mm(acat, picked).astype(BF16)


def dense_forward(x, agg, cot, ws, wn, wo):
    pre = mm(x, ws) + mm(agg, wn)
    sigma = jax.nn.sigmoid(pre)
    act = (pre * sigma).astype(BF16)
    d_pre = (mm_bt(cot, wo) * sigma * (1.0 + pre * (1.0 - sigma))).astype(BF16)
    return act, d_pre


def add_grads(g_ref, x, agg, act, cot, d_pre, fresh):
    hidden = d_pre.shape[1]
    for p, part in enumerate((mm_at(x, d_pre), mm_at(agg, d_pre), mm_at(act, cot))):
        sl = slice(p * hidden, (p + 1) * hidden)
        if fresh:
            g_ref[sl, :] = part
        else:
            g_ref[sl, :] += part


def send_rows(acc_ref, acat_ref, da_ref, cols, slots):
    clones, _, hidden = acc_ref.shape
    size = acat_ref.shape[1]
    for r in range(R):
        msg = mm_at(acat_ref[r], da_ref[r * size : (r + 1) * size, :])
        for k in range(slots):
            at = block_at(cols(r, k), size)
            for c in range(clones):
                acc_ref[c, at, :] += msg[k * size : (k + 1) * size, c * hidden : (c + 1) * hidden]


def whole_chunk(a_ref, cot_ref, xe, acc, g, upd_ref, acat_s, agg_s, da_s, ws, wn, wo, base, cols, live, fresh, late=()):
    clones, width, hidden = cot_ref.shape
    slots, size = a_ref.shape[1:3]
    rows = pl.ds(pl.multiple_of((base + R) * size, width), width)
    aggregate_rows(a_ref, acat_s, agg_s, xe, cols, live)
    wait_all(late)
    for c in range(clones):
        x, agg, cot = xe[c, rows, :], agg_s[c], cot_ref[c]
        act, d_pre = dense_forward(x, agg, cot, ws[...], wn[...], wo[...])
        upd_ref[c] = (x.astype(F32) + mm(act, wo[...])).astype(BF16)
        add_grads(g, x, agg, act, cot, d_pre, fresh and c == 0)
        da_s[:, c * hidden : (c + 1) * hidden] = mm_bt(d_pre, wn[...]).astype(BF16)
        acc[c, rows, :] += cot.astype(F32) + mm_bt(d_pre, ws[...])
    send_rows(acc, acat_s, da_s, cols, slots)


def mid_kernel(
    idx, cols_ref, cnt_ref, x_hbm, a_hbm, cot_hbm, ws_hbm, wn_hbm, wo_hbm,
    upd_hbm, xe, acc, g, a_near, a_far, cot_near, cot_far, ws, wn, wo,
    a_s, cot_s, upd_s, acat_s, agg_s, da_s, sems,
):
    clones, rows, hidden = x_hbm.shape
    per, slots, size, _ = a_hbm.shape
    width = R * size
    chunks = per // R - 2
    odd = lax.rem(idx[0], 2) == 1
    first = idx[0] * per - R
    near = jnp.where(odd, 0, per - R)
    far = jnp.where(odd, per - R, 0)
    count = iter(range(100))

    def load(source, target):
        copy = pltpu.make_async_copy(source, target, sems.at[next(count)])
        copy.start()
        return copy

    def rows_of(ref, row):
        return ref.at[:, pl.ds(pl.multiple_of(row * size, width), width), :]

    a_in, cot_in, x_in = [], [], []
    x_in.append([load(x_hbm.at[:, : 3 * width, :], xe.at[:, width : 4 * width, :])])
    for i in range(chunks):
        a_in.append(load(a_hbm.at[R + R * i : 2 * R + R * i], a_s.at[i]))
        cot_in.append(load(rows_of(cot_hbm, R + R * i), cot_s.at[i]))
        if i > 0:
            lo, hi = (i + 2) * width, (i + 3) * width
            x_in.append([load(x_hbm.at[:, lo:hi, :], xe.at[:, lo + width : hi + width, :])])
        if i == 0:
            weights = [load(*pair) for pair in ((ws_hbm, ws), (wn_hbm, wn), (wo_hbm, wo))]
    late = [
        load(a_hbm.at[pl.ds(near, R)], a_near),
        load(rows_of(cot_hbm, near), cot_near),
        load(a_hbm.at[pl.ds(far, R)], a_far),
        load(rows_of(cot_hbm, far), cot_far),
    ]
    acc[...] = jnp.zeros_like(acc)
    for i in range(chunks):
        base = R + R * i
        wait_all(x_in[i] + [a_in[i]])
        whole_chunk(
            a_s.at[i], cot_s.at[i], xe, acc, g, upd_s.at[i], acat_s, agg_s, da_s, ws, wn, wo, base,
            lambda r, k: cols_ref[k, base + r] - first, lambda r: cnt_ref[base + r], i == 0,
            [cot_in[i]] + (weights if i == 0 else []),
        )
        late.append(load(upd_s.at[i], rows_of(upd_hbm, base)))
    wait_all(late)


def near_kernel(
    idx, cols_ref, cnt_ref, halo, a_ref, cot_ref, ws, wn, wo, upd_in, xe_in, acc_in, g_in,
    upd_hbm, xe, acc, g, msg_ref,
    upd_s, acat_s, agg_s, da_s, sem,
):
    clones, width, hidden = halo.shape
    size = a_ref.shape[2]
    per = xe.shape[1] // size - 2 * R
    odd = lax.rem(idx[0], 2) == 1
    first = idx[0] * per - R
    base = jnp.where(odd, 0, per - R)
    outer = pl.ds(pl.multiple_of(jnp.where(odd, 0, R + per) * size, width), width)
    xe[:, outer, :] = halo[...]
    whole_chunk(
        a_ref, cot_ref, xe, acc, g, upd_s, acat_s, agg_s, da_s, ws, wn, wo, base,
        lambda r, k: cols_ref[k, base + r] - first, lambda r: cnt_ref[base + r], False,
    )
    store = pltpu.make_async_copy(
        upd_s, upd_hbm.at[:, pl.ds(pl.multiple_of(base * size, width), width), :], sem
    )
    store.start()
    msg_ref[...] = acc[:, outer, :].astype(BF16)
    store.wait()


def far_kernel(
    idx, cols_ref, cnt_ref, halo, a_ref, cot_ref, ws, wn, wo, xe_in, g_in,
    xe, keep_ref, send_ref, act_ref, dpre_ref, acat_ref,
    agg_s, g_s,
):
    clones, width, hidden = halo.shape
    size = a_ref.shape[2]
    per = xe.shape[1] // size - 2 * R
    odd = lax.rem(idx[0], 2)
    first = idx[0] * per - R
    base = jnp.where(odd == 1, per - R, 0)
    outer = pl.ds(pl.multiple_of(jnp.where(odd == 1, R + per, 0) * size, width), width)
    rows = pl.ds(pl.multiple_of((base + R) * size, width), width)
    xe[:, outer, :] = halo[...]
    aggregate_rows(
        a_ref, acat_ref, agg_s, xe,
        lambda r, k: cols_ref[k, base + r] - first, lambda r: cnt_ref[base + r],
    )
    g_s[...] = g_in[...]
    for c in range(clones):
        x, agg, cot = xe[c, rows, :], agg_s[c], cot_ref[c]
        act, d_pre = dense_forward(x, agg, cot, ws[...], wn[...], wo[...])
        act_ref[c] = act
        dpre_ref[c] = d_pre
        add_grads(g_s, x, agg, act, cot, d_pre, False)
    half = g_s.shape[0] // 2
    keep_ref[...] = g_s[pl.ds(pl.multiple_of(odd * half, half), half), :]
    send_ref[...] = g_s[pl.ds(pl.multiple_of((1 - odd) * half, half), half), :]


def message_kernel(idx, cols_ref, dpre, acat, wn, acc_in, acc, msg_ref, da_s):
    clones, width, hidden = dpre.shape
    size = acat.shape[1]
    per = acc.shape[1] // size - 2 * R
    odd = lax.rem(idx[0], 2) == 1
    first = idx[0] * per - R
    base = jnp.where(odd, per - R, 0)
    outer = pl.ds(pl.multiple_of(jnp.where(odd, R + per, 0) * size, width), width)
    for c in range(clones):
        da_s[:, c * hidden : (c + 1) * hidden] = mm_bt(dpre[c], wn[...]).astype(BF16)
    send_rows(acc, acat, da_s, lambda r, k: cols_ref[k, base + r] - first, acat.shape[2] // size)
    msg_ref[...] = acc[:, outer, :].astype(BF16)


def own_kernel(
    idx, nrecv, act, dpre, cot_ref, xe, acc, ws, wo, upd_in,
    upd_hbm, grad_hbm, edge_ref,
    upd_s, grad_s, sems,
):
    clones, width, hidden = act.shape
    rows = upd_hbm.shape[1]
    odd = lax.rem(idx[0], 2) == 1
    far = pl.multiple_of(jnp.where(odd, rows - width, 0), width)
    near = pl.multiple_of(jnp.where(odd, 0, rows - width), width)
    copies = []

    def store(source, target):
        copies.append(pltpu.make_async_copy(source, target, sems.at[len(copies)]))
        copies[-1].start()

    inner = rows - 2 * width
    grad_s[:, :inner, :] = acc[:, 2 * width : 2 * width + inner, :].astype(BF16)
    store(grad_s.at[:, pl.ds(0, inner), :], grad_hbm.at[:, pl.ds(width, inner), :])
    grad_s[:, inner:, :] = (
        acc[:, pl.ds(near + width, width), :] + nrecv[...].astype(F32)
    ).astype(BF16)
    store(grad_s.at[:, pl.ds(inner, width), :], grad_hbm.at[:, pl.ds(near, width), :])
    for c in range(clones):
        x = xe[c, pl.ds(far + width, width), :]
        upd_s[c] = (x.astype(F32) + mm(act[c], wo[...])).astype(BF16)
    store(upd_s, upd_hbm.at[:, pl.ds(far, width), :])
    for c in range(clones):
        edge_ref[c] = (
            acc[c, pl.ds(far + width, width), :] + cot_ref[c].astype(F32) + mm_bt(dpre[c], ws[...])
        )
    wait_all(copies)


def edge_kernel(idx, edge_ref, frecv_ref, grad_in, grad_hbm, out_s, sem):
    rows, width = grad_hbm.shape[1], edge_ref.shape[1]
    start = pl.multiple_of(jnp.where(lax.rem(idx[0], 2) == 1, rows - width, 0), width)
    out_s[...] = (edge_ref[...] + frecv_ref[...].astype(F32)).astype(BF16)
    out = pltpu.make_async_copy(out_s, grad_hbm.at[:, pl.ds(start, width), :], sem)
    out.start()
    out.wait()


def swap(value, bit):
    count = lax.axis_size("dom")
    return lax.ppermute(value, "dom", [(i, i ^ bit) for i in range(count)])


def half_rows(ref, bit):
    half = ref.shape[0] // 2
    return pl.ds(pl.multiple_of(bit * half, half), half)


def bit_of(idx, shift):
    return lax.rem(lax.shift_right_logical(idx[0], shift), 2)


def scatter_kernel(shift, idx, mine, other, keep_ref, send_ref):
    bit = bit_of(idx, shift)
    stay, leave = half_rows(mine, bit), half_rows(mine, 1 - bit)
    send_ref[...] = (mine[leave, :] + other[leave, :].astype(F32)).astype(BF16)
    keep_ref[...] = mine[stay, :] + other[stay, :].astype(F32)


def add_kernel(mine, other, out_ref):
    out_ref[...] = (mine[...].astype(F32) + other[...].astype(F32)).astype(BF16)


def join_kernel(shift, idx, mine, other, out_ref):
    bit = bit_of(idx, shift)
    out_ref[half_rows(out_ref, bit), :] = mine[...]
    out_ref[half_rows(out_ref, 1 - bit), :] = other[...]


def final_kernel(factor, idx, mine, other, gs_ref, gn_ref, go_ref, all_s):
    join_kernel(0, idx, mine, other, all_s)
    hidden = gs_ref.shape[0]
    for p, ref in enumerate((gs_ref, gn_ref, go_ref)):
        ref[...] = all_s[p * hidden : (p + 1) * hidden, :].astype(F32) * factor


def reduce_all(call, keep, send, idx, factor, hooks):
    count = lax.axis_size("dom")
    hidden = keep.shape[1]
    stage = iter(range(100))
    sds = jax.ShapeDtypeStruct

    def vm(rows, kind):
        return pltpu.VMEM((rows, hidden), kind)

    def exchange(value, shift):
        moved = swap(value, 1 << shift)
        for hook in hooks.get(next(stage), ()):
            moved = hook(value, moved)
        return in_vmem(moved)

    mine, other = keep, exchange(send, 0)
    shifts = list(range(1, count.bit_length() - 1))
    scatter = shifts[1:2]
    for shift in scatter:
        rows = mine.shape[0] // 2
        mine, out = call(
            functools.partial(scatter_kernel, shift), "scatter", (idx, mine, other),
            [SM, VM, VM], (vm(rows, F32), vm(rows, BF16)), (VM, VM), [],
        )
        other = exchange(out, shift)
    for shift in [None] + [s for s in reversed(shifts) if s not in scatter]:
        if shift is not None:
            other = exchange(mine, shift)
        mine = call(add_kernel, "add", (mine, other), [VM, VM], vm(mine.shape[0], BF16), VM, [])
    for shift in reversed(scatter):
        other = exchange(mine, shift)
        mine = call(
            functools.partial(join_kernel, shift), "join", (idx, mine, other),
            [SM, VM, VM], vm(2 * mine.shape[0], BF16), VM, [],
        )
    other = exchange(mine, 0)
    return call(
        functools.partial(final_kernel, factor), "final", (idx, mine, other),
        [SM, VM, VM], (sds((hidden, hidden), F32),) * 3, (VM,) * 3, [vm(3 * hidden, BF16)],
    )


def body(features, cotangent, adjacency, tile_cols, tile_counts, w_self, w_neigh, w_out):
    clones, rows, hidden = features.shape
    per, slots, size, _ = adjacency.shape
    width = R * size
    chunks = per // R - 2
    count = lax.axis_size("dom")
    index = lax.axis_index("dom")
    odd = (index & 1) == 1
    idx = index.reshape(1).astype(jnp.int32)
    cols = tile_cols.T
    near_pairs = [(i, i ^ 1) for i in range(count)]
    far_pairs = [(i, ((i + 1) ^ 1) - 1) for i in range(1, count - 1)]
    far_out = lax.dynamic_slice_in_dim(features, jnp.where(odd, rows - width, 0), width, axis=1)
    far_halo = lax.ppermute(far_out, "dom", far_pairs)
    near_out = lax.dynamic_slice_in_dim(features, jnp.where(odd, 0, rows - width), width, axis=1)
    near_halo = lax.ppermute(near_out, "dom", near_pairs)

    sds = jax.ShapeDtypeStruct
    full = sds((clones, rows, hidden), BF16)
    strip = pltpu.VMEM((clones, width, hidden), BF16)
    xe_t = pltpu.VMEM((clones, rows + 2 * width, hidden), BF16)
    acc_t = pltpu.VMEM((clones, rows + 2 * width, hidden), F32)
    g_t = pltpu.VMEM((3 * hidden, hidden), F32)
    half_t = pltpu.VMEM((3 * hidden // 2, hidden), F32)
    a_t = pltpu.VMEM((R, slots, size, size), BF16)
    acat_t = pltpu.VMEM((R, size, slots * size), BF16)
    da_t = pltpu.VMEM((width, clones * hidden), BF16)

    def call(kernel, name, ins, in_specs, outs, out_specs, scratch, aliases=None):
        return pl.pallas_call(
            kernel,
            out_shape=outs,
            in_specs=in_specs,
            out_specs=out_specs,
            scratch_shapes=scratch,
            input_output_aliases=aliases or {},
            compiler_params=pltpu.CompilerParams(vmem_limit_bytes=LIMIT),
            cost_estimate=pl.CostEstimate(flops=COSTS.get(name, 1), transcendentals=0, bytes_accessed=0),
            name=name,
        )(*ins)

    w_t = pltpu.VMEM((hidden, hidden), BF16)
    big = tuple(in_hbm(v) for v in (features, adjacency, cotangent, w_self, w_neigh, w_out))
    upd, xe, acc, g, a_near, a_far, cot_near, cot_far, ws, wn, wo = call(
        mid_kernel, "mid_rows",
        (idx, cols, tile_counts) + big,
        [SM] * 3 + [ANY] * 6,
        (full, xe_t, acc_t, g_t, a_t, a_t, strip, strip, w_t, w_t, w_t),
        (ANY,) + (VM,) * 10,
        [
            pltpu.VMEM((chunks, R, slots, size, size), BF16),
            pltpu.VMEM((chunks, clones, width, hidden), BF16),
            pltpu.VMEM((chunks, clones, width, hidden), BF16),
            acat_t, strip, da_t,
            pltpu.SemaphoreType.DMA((4 * chunks + 7,)),
        ],
    )
    upd, xe, acc, g, near_msg = call(
        near_kernel, "near_rows",
        (idx, cols, tile_counts, in_vmem(near_halo), a_near, cot_near, ws, wn, wo, upd, xe, acc, g),
        [SM] * 3 + [VM] * 6 + [ANY] + [VM] * 3,
        (full, xe_t, acc_t, g_t, strip),
        (ANY,) + (VM,) * 4,
        [strip, acat_t, strip, da_t, pltpu.SemaphoreType.DMA],
        {9: 0, 10: 1, 11: 2, 12: 3},
    )
    near_recv = lax.ppermute(near_msg, "dom", near_pairs)
    xe, keep, send, act, d_pre, acat = call(
        far_kernel, "far_rows",
        (idx, cols, tile_counts, in_vmem(far_halo), a_far, cot_far, ws, wn, wo, xe, g),
        [SM] * 3 + [VM] * 8,
        (xe_t, half_t, half_t, strip, strip, acat_t),
        (VM,) * 6,
        [strip, g_t],
        {9: 0},
    )
    kept = {}

    def held(value, before):
        value, before = lax.optimization_barrier((value, before))
        return value, before

    def message(after, before):
        gate, _ = lax.optimization_barrier((idx, after))
        kept["acc"], msg = call(
            message_kernel, "messages",
            (gate, cols, d_pre, acat, wn, acc),
            [SM] * 2 + [VM] * 4,
            (acc_t, strip),
            (VM, VM),
            [da_t],
            {5: 0},
        )
        kept["msg"], before = held(msg, before)
        return before

    def far_send(after, before):
        msg, _ = lax.optimization_barrier((kept["msg"], after))
        kept["recv"] = lax.ppermute(msg, "dom", far_pairs)
        return before

    def own(after, before):
        gate, _ = lax.optimization_barrier((idx, after))
        kept["upd"], grad, kept["edge"] = call(
            own_kernel, "own_rows",
            (gate, in_vmem(near_recv), act, d_pre, cot_far, xe, kept["acc"], ws, wo, upd),
            [SM] + [VM] * 8 + [ANY],
            (full, full, pltpu.VMEM((clones, width, hidden), F32)),
            (ANY, ANY, VM),
            [strip, pltpu.VMEM((clones, rows - width, hidden), BF16), pltpu.SemaphoreType.DMA((3,))],
            {9: 0},
        )
        kept["grad"], before = held(grad, before)
        return before

    def edge(after, before):
        gate, _ = lax.optimization_barrier((idx, after))
        grad = call(
            edge_kernel, "edge_rows",
            (gate, kept["edge"], in_vmem(kept["recv"]), kept["grad"]),
            [SM, VM, VM, ANY],
            full,
            ANY,
            [strip, pltpu.SemaphoreType.DMA],
            {3: 0},
        )
        kept["grad"], before = held(grad, before)
        return before

    factor = 1.0 / math.sqrt(2.0 * rows * count)
    hooks = {0: (message,), 1: (far_send,)}
    for at, hook in ((OWN_AT, own), (EDGE_AT, edge)):
        hooks[at] = hooks.get(at, ()) + (hook,)
    sums = reduce_all(call, keep, send, idx, factor, hooks)
    return (
        kept["upd"],
        kept["grad"],
        *sums,
    )


def solution(mesh):
    return jax.shard_map(
        body,
        mesh=mesh,
        in_specs=(
            P("groups", "dom", None),
            P("groups", "dom", None),
            P("dom", None, None, None),
            P("dom", None),
            P("dom"),
            P(),
            P(),
            P(),
        ),
        out_specs=(
            P("groups", "dom", None),
            P("groups", "dom", None),
            P("groups", None),
            P("groups", None),
            P("groups", None),
        ),
        check_vma=False,
    )
```

```python
import functools
import math

import jax
import jax.numpy as jnp
from jax import lax
from jax.experimental import pallas as pl
from jax.experimental.pallas import tpu as pltpu
from jax.sharding import PartitionSpec as P

R = 4
F32 = jnp.float32
BF16 = jnp.bfloat16
ANY = pl.BlockSpec(memory_space=pltpu.HBM)
VM = pl.BlockSpec(memory_space=pltpu.VMEM)
SM = pl.BlockSpec(memory_space=pltpu.SMEM)
OWN_AT, EDGE_AT = 2, 4
COSTS = dict(mid_rows=1, near_rows=1, far_rows=1, messages=1, own_rows=1, edge_rows=1)
LIMIT = 12 * 1024 * 1024


def mm(a, b):
    return lax.dot_general(a, b, (((1,), (0,)), ((), ())), preferred_element_type=F32)


def mm_bt(a, b):
    return lax.dot_general(a, b, (((1,), (1,)), ((), ())), preferred_element_type=F32)


def mm_at(a, b):
    return lax.dot_general(a, b, (((0,), (0,)), ((), ())), preferred_element_type=F32)


def block_at(index, size):
    return pl.ds(pl.multiple_of(index * size, size), size)


def start_all(copies):
    for copy in copies:
        copy.start()
    return copies


def wait_all(copies):
    for copy in copies:
        copy.wait()


def in_vmem(value):
    return pltpu.with_memory_space_constraint(value, pltpu.VMEM)


def in_hbm(value):
    return pltpu.with_memory_space_constraint(value, pltpu.HBM)


def aggregate_rows(a_ref, acat_ref, agg_ref, x_ref, cols, live):
    slots, size = a_ref.shape[1:3]
    for r in range(R):
        acat = jnp.concatenate(
            [jnp.where(k < live(r), a_ref[r, k], jnp.zeros((), BF16)) for k in range(slots)], axis=1
        )
        acat_ref[r] = acat
        for c in range(x_ref.shape[0]):
            picked = jnp.concatenate(
                [x_ref[c, block_at(cols(r, k), size), :] for k in range(slots)], axis=0
            )
            agg_ref[c, r * size : (r + 1) * size, :] = mm(acat, picked).astype(BF16)


def dense_forward(x, agg, cot, ws, wn, wo):
    pre = mm(x, ws) + mm(agg, wn)
    sigma = jax.nn.sigmoid(pre)
    act = (pre * sigma).astype(BF16)
    d_pre = (mm_bt(cot, wo) * sigma * (1.0 + pre * (1.0 - sigma))).astype(BF16)
    return act, d_pre


def add_grads(g_ref, x, agg, act, cot, d_pre, fresh):
    hidden = d_pre.shape[1]
    for p, part in enumerate((mm_at(x, d_pre), mm_at(agg, d_pre), mm_at(act, cot))):
        sl = slice(p * hidden, (p + 1) * hidden)
        if fresh:
            g_ref[sl, :] = part
        else:
            g_ref[sl, :] += part


def send_rows(acc_ref, acat_ref, da_ref, cols, slots):
    clones, _, hidden = acc_ref.shape
    size = acat_ref.shape[1]
    for r in range(R):
        msg = mm_at(acat_ref[r], da_ref[r * size : (r + 1) * size, :])
        for k in range(slots):
            at = block_at(cols(r, k), size)
            for c in range(clones):
                acc_ref[c, at, :] += msg[k * size : (k + 1) * size, c * hidden : (c + 1) * hidden]


def whole_chunk(a_ref, cot_ref, xe, acc, g, upd_ref, acat_s, agg_s, da_s, ws, wn, wo, base, cols, live, fresh, late=()):
    clones, width, hidden = cot_ref.shape
    slots, size = a_ref.shape[1:3]
    rows = pl.ds(pl.multiple_of((base + R) * size, width), width)
    aggregate_rows(a_ref, acat_s, agg_s, xe, cols, live)
    wait_all(late)
    for c in range(clones):
        x, agg, cot = xe[c, rows, :], agg_s[c], cot_ref[c]
        act, d_pre = dense_forward(x, agg, cot, ws[...], wn[...], wo[...])
        upd_ref[c] = (x.astype(F32) + mm(act, wo[...])).astype(BF16)
        add_grads(g, x, agg, act, cot, d_pre, fresh and c == 0)
        da_s[:, c * hidden : (c + 1) * hidden] = mm_bt(d_pre, wn[...]).astype(BF16)
        acc[c, rows, :] += cot.astype(F32) + mm_bt(d_pre, ws[...])
    send_rows(acc, acat_s, da_s, cols, slots)


def mid_kernel(
    idx, cols_ref, cnt_ref, x_hbm, a_hbm, cot_hbm, ws_hbm, wn_hbm, wo_hbm,
    upd_hbm, xe, acc, g, a_near, a_far, cot_near, cot_far, ws, wn, wo,
    a_s, cot_s, upd_s, acat_s, agg_s, da_s, sems,
):
    clones, rows, hidden = x_hbm.shape
    per, slots, size, _ = a_hbm.shape
    width = R * size
    chunks = per // R - 2
    odd = lax.rem(idx[0], 2) == 1
    first = idx[0] * per - R
    near = jnp.where(odd, 0, per - R)
    far = jnp.where(odd, per - R, 0)
    count = iter(range(100))

    def load(source, target):
        copy = pltpu.make_async_copy(source, target, sems.at[next(count)])
        copy.start()
        return copy

    def rows_of(ref, row):
        return ref.at[:, pl.ds(pl.multiple_of(row * size, width), width), :]

    a_in, cot_in, x_in = [], [], []
    x_in.append([load(x_hbm.at[:, : 3 * width, :], xe.at[:, width : 4 * width, :])])
    for i in range(chunks):
        a_in.append(load(a_hbm.at[R + R * i : 2 * R + R * i], a_s.at[i]))
        cot_in.append(load(rows_of(cot_hbm, R + R * i), cot_s.at[i]))
        if i > 0:
            lo, hi = (i + 2) * width, (i + 3) * width
            x_in.append([load(x_hbm.at[:, lo:hi, :], xe.at[:, lo + width : hi + width, :])])
        if i == 0:
            weights = [load(*pair) for pair in ((ws_hbm, ws), (wn_hbm, wn), (wo_hbm, wo))]
    late = [
        load(a_hbm.at[pl.ds(near, R)], a_near),
        load(rows_of(cot_hbm, near), cot_near),
        load(a_hbm.at[pl.ds(far, R)], a_far),
        load(rows_of(cot_hbm, far), cot_far),
    ]
    acc[...] = jnp.zeros_like(acc)
    for i in range(chunks):
        base = R + R * i
        wait_all(x_in[i] + [a_in[i]])
        whole_chunk(
            a_s.at[i], cot_s.at[i], xe, acc, g, upd_s.at[i], acat_s, agg_s, da_s, ws, wn, wo, base,
            lambda r, k: cols_ref[k, base + r] - first, lambda r: cnt_ref[base + r], i == 0,
            [cot_in[i]] + (weights if i == 0 else []),
        )
        late.append(load(upd_s.at[i], rows_of(upd_hbm, base)))
    wait_all(late)


def near_kernel(
    idx, cols_ref, cnt_ref, halo, a_ref, cot_ref, ws, wn, wo, upd_in, xe_in, acc_in, g_in,
    upd_hbm, xe, acc, g, msg_ref,
    upd_s, acat_s, agg_s, da_s, sem,
):
    clones, width, hidden = halo.shape
    size = a_ref.shape[2]
    per = xe.shape[1] // size - 2 * R
    odd = lax.rem(idx[0], 2) == 1
    first = idx[0] * per - R
    base = jnp.where(odd, 0, per - R)
    outer = pl.ds(pl.multiple_of(jnp.where(odd, 0, R + per) * size, width), width)
    xe[:, outer, :] = halo[...]
    whole_chunk(
        a_ref, cot_ref, xe, acc, g, upd_s, acat_s, agg_s, da_s, ws, wn, wo, base,
        lambda r, k: cols_ref[k, base + r] - first, lambda r: cnt_ref[base + r], False,
    )
    store = pltpu.make_async_copy(
        upd_s, upd_hbm.at[:, pl.ds(pl.multiple_of(base * size, width), width), :], sem
    )
    store.start()
    msg_ref[...] = acc[:, outer, :].astype(BF16)
    store.wait()


def far_kernel(
    idx, cols_ref, cnt_ref, halo, a_ref, cot_ref, ws, wn, wo, xe_in, g_in,
    xe, keep_ref, send_ref, act_ref, dpre_ref, acat_ref,
    agg_s, g_s,
):
    clones, width, hidden = halo.shape
    size = a_ref.shape[2]
    per = xe.shape[1] // size - 2 * R
    odd = lax.rem(idx[0], 2)
    first = idx[0] * per - R
    base = jnp.where(odd == 1, per - R, 0)
    outer = pl.ds(pl.multiple_of(jnp.where(odd == 1, R + per, 0) * size, width), width)
    rows = pl.ds(pl.multiple_of((base + R) * size, width), width)
    xe[:, outer, :] = halo[...]
    aggregate_rows(
        a_ref, acat_ref, agg_s, xe,
        lambda r, k: cols_ref[k, base + r] - first, lambda r: cnt_ref[base + r],
    )
    g_s[...] = g_in[...]
    for c in range(clones):
        x, agg, cot = xe[c, rows, :], agg_s[c], cot_ref[c]
        act, d_pre = dense_forward(x, agg, cot, ws[...], wn[...], wo[...])
        act_ref[c] = act
        dpre_ref[c] = d_pre
        add_grads(g_s, x, agg, act, cot, d_pre, False)
    half = g_s.shape[0] // 2
    keep_ref[...] = g_s[pl.ds(pl.multiple_of(odd * half, half), half), :]
    send_ref[...] = g_s[pl.ds(pl.multiple_of((1 - odd) * half, half), half), :]


def message_kernel(idx, cols_ref, dpre, acat, wn, acc_in, acc, msg_ref, da_s):
    clones, width, hidden = dpre.shape
    size = acat.shape[1]
    per = acc.shape[1] // size - 2 * R
    odd = lax.rem(idx[0], 2) == 1
    first = idx[0] * per - R
    base = jnp.where(odd, per - R, 0)
    outer = pl.ds(pl.multiple_of(jnp.where(odd, R + per, 0) * size, width), width)
    for c in range(clones):
        da_s[:, c * hidden : (c + 1) * hidden] = mm_bt(dpre[c], wn[...]).astype(BF16)
    send_rows(acc, acat, da_s, lambda r, k: cols_ref[k, base + r] - first, acat.shape[2] // size)
    msg_ref[...] = acc[:, outer, :].astype(BF16)


def own_kernel(
    idx, nrecv, act, dpre, cot_ref, xe, acc, ws, wo, upd_in,
    upd_hbm, grad_hbm, edge_ref,
    upd_s, grad_s, sems,
):
    clones, width, hidden = act.shape
    rows = upd_hbm.shape[1]
    odd = lax.rem(idx[0], 2) == 1
    far = pl.multiple_of(jnp.where(odd, rows - width, 0), width)
    near = pl.multiple_of(jnp.where(odd, 0, rows - width), width)
    copies = []

    def store(source, target):
        copies.append(pltpu.make_async_copy(source, target, sems.at[len(copies)]))
        copies[-1].start()

    inner = rows - 2 * width
    grad_s[:, :inner, :] = acc[:, 2 * width : 2 * width + inner, :].astype(BF16)
    store(grad_s.at[:, pl.ds(0, inner), :], grad_hbm.at[:, pl.ds(width, inner), :])
    grad_s[:, inner:, :] = (
        acc[:, pl.ds(near + width, width), :] + nrecv[...].astype(F32)
    ).astype(BF16)
    store(grad_s.at[:, pl.ds(inner, width), :], grad_hbm.at[:, pl.ds(near, width), :])
    for c in range(clones):
        x = xe[c, pl.ds(far + width, width), :]
        upd_s[c] = (x.astype(F32) + mm(act[c], wo[...])).astype(BF16)
    store(upd_s, upd_hbm.at[:, pl.ds(far, width), :])
    for c in range(clones):
        edge_ref[c] = (
            acc[c, pl.ds(far + width, width), :] + cot_ref[c].astype(F32) + mm_bt(dpre[c], ws[...])
        )
    wait_all(copies)


def edge_kernel(idx, edge_ref, straight_ref, across_ref, grad_in, grad_hbm, out_s, sem):
    rows, width = grad_hbm.shape[1], edge_ref.shape[1]
    start = pl.multiple_of(jnp.where(lax.rem(idx[0], 2) == 1, rows - width, 0), width)
    received = straight_ref[...].astype(F32) + across_ref[...].astype(F32)
    out_s[...] = (edge_ref[...] + received).astype(BF16)
    out = pltpu.make_async_copy(out_s, grad_hbm.at[:, pl.ds(start, width), :], sem)
    out.start()
    out.wait()


def swap(value, bit):
    count = lax.axis_size("dom")
    return lax.ppermute(value, "dom", [(i, i ^ bit) for i in range(count)])


def half_rows(ref, bit):
    half = ref.shape[0] // 2
    return pl.ds(pl.multiple_of(bit * half, half), half)


def bit_of(idx, shift):
    return lax.rem(lax.shift_right_logical(idx[0], shift), 2)


def scatter_kernel(shift, idx, mine, other, keep_ref, send_ref):
    bit = bit_of(idx, shift)
    stay, leave = half_rows(mine, bit), half_rows(mine, 1 - bit)
    send_ref[...] = (mine[leave, :] + other[leave, :].astype(F32)).astype(BF16)
    keep_ref[...] = mine[stay, :] + other[stay, :].astype(F32)


def add_kernel(mine, other, out_ref):
    out_ref[...] = (mine[...].astype(F32) + other[...].astype(F32)).astype(BF16)


def join_kernel(shift, idx, mine, other, out_ref):
    bit = bit_of(idx, shift)
    out_ref[half_rows(out_ref, bit), :] = mine[...]
    out_ref[half_rows(out_ref, 1 - bit), :] = other[...]


def final_kernel(factor, idx, mine, other, gs_ref, gn_ref, go_ref, all_s):
    join_kernel(0, idx, mine, other, all_s)
    hidden = gs_ref.shape[0]
    for p, ref in enumerate((gs_ref, gn_ref, go_ref)):
        ref[...] = all_s[p * hidden : (p + 1) * hidden, :].astype(F32) * factor


def reduce_all(call, keep, send, idx, factor, hooks):
    count = lax.axis_size("dom")
    hidden = keep.shape[1]
    stage = iter(range(100))
    sds = jax.ShapeDtypeStruct

    def vm(rows, kind):
        return pltpu.VMEM((rows, hidden), kind)

    def exchange(value, shift):
        moved = swap(value, 1 << shift)
        for hook in hooks.get(next(stage), ()):
            moved = hook(value, moved)
        return in_vmem(moved)

    mine, other = keep, exchange(send, 0)
    shifts = list(range(1, count.bit_length() - 1))
    scatter = shifts[1:2]
    for shift in scatter:
        rows = mine.shape[0] // 2
        mine, out = call(
            functools.partial(scatter_kernel, shift), "scatter", (idx, mine, other),
            [SM, VM, VM], (vm(rows, F32), vm(rows, BF16)), (VM, VM), [],
        )
        other = exchange(out, shift)
    for shift in [None] + [s for s in reversed(shifts) if s not in scatter]:
        if shift is not None:
            other = exchange(mine, shift)
        mine = call(add_kernel, "add", (mine, other), [VM, VM], vm(mine.shape[0], BF16), VM, [])
    for shift in reversed(scatter):
        other = exchange(mine, shift)
        mine = call(
            functools.partial(join_kernel, shift), "join", (idx, mine, other),
            [SM, VM, VM], vm(2 * mine.shape[0], BF16), VM, [],
        )
    other = exchange(mine, 0)
    return call(
        functools.partial(final_kernel, factor), "final", (idx, mine, other),
        [SM, VM, VM], (sds((hidden, hidden), F32),) * 3, (VM,) * 3, [vm(3 * hidden, BF16)],
    )


def body(features, cotangent, adjacency, tile_cols, tile_counts, w_self, w_neigh, w_out):
    clones, rows, hidden = features.shape
    per, slots, size, _ = adjacency.shape
    width = R * size
    chunks = per // R - 2
    count = lax.axis_size("dom")
    index = lax.axis_index("dom")
    odd = (index & 1) == 1
    idx = index.reshape(1).astype(jnp.int32)
    cols = tile_cols.T
    near_pairs = [(i, i ^ 1) for i in range(count)]
    far_pairs = [(i, ((i + 1) ^ 1) - 1) for i in range(1, count - 1)]
    far_out = lax.dynamic_slice_in_dim(features, jnp.where(odd, rows - width, 0), width, axis=1)
    far_halo = lax.ppermute(far_out, "dom", far_pairs)
    near_out = lax.dynamic_slice_in_dim(features, jnp.where(odd, 0, rows - width), width, axis=1)
    near_halo = lax.ppermute(near_out, "dom", near_pairs)

    sds = jax.ShapeDtypeStruct
    full = sds((clones, rows, hidden), BF16)
    strip = pltpu.VMEM((clones, width, hidden), BF16)
    xe_t = pltpu.VMEM((clones, rows + 2 * width, hidden), BF16)
    acc_t = pltpu.VMEM((clones, rows + 2 * width, hidden), F32)
    g_t = pltpu.VMEM((3 * hidden, hidden), F32)
    half_t = pltpu.VMEM((3 * hidden // 2, hidden), F32)
    a_t = pltpu.VMEM((R, slots, size, size), BF16)
    acat_t = pltpu.VMEM((R, size, slots * size), BF16)
    da_t = pltpu.VMEM((width, clones * hidden), BF16)

    def call(kernel, name, ins, in_specs, outs, out_specs, scratch, aliases=None):
        return pl.pallas_call(
            kernel,
            out_shape=outs,
            in_specs=in_specs,
            out_specs=out_specs,
            scratch_shapes=scratch,
            input_output_aliases=aliases or {},
            compiler_params=pltpu.CompilerParams(vmem_limit_bytes=LIMIT),
            cost_estimate=pl.CostEstimate(flops=COSTS.get(name, 1), transcendentals=0, bytes_accessed=0),
            name=name,
        )(*ins)

    w_t = pltpu.VMEM((hidden, hidden), BF16)
    big = tuple(in_hbm(v) for v in (features, adjacency, cotangent, w_self, w_neigh, w_out))
    upd, xe, acc, g, a_near, a_far, cot_near, cot_far, ws, wn, wo = call(
        mid_kernel, "mid_rows",
        (idx, cols, tile_counts) + big,
        [SM] * 3 + [ANY] * 6,
        (full, xe_t, acc_t, g_t, a_t, a_t, strip, strip, w_t, w_t, w_t),
        (ANY,) + (VM,) * 10,
        [
            pltpu.VMEM((chunks, R, slots, size, size), BF16),
            pltpu.VMEM((chunks, clones, width, hidden), BF16),
            pltpu.VMEM((chunks, clones, width, hidden), BF16),
            acat_t, strip, da_t,
            pltpu.SemaphoreType.DMA((4 * chunks + 7,)),
        ],
    )
    upd, xe, acc, g, near_msg = call(
        near_kernel, "near_rows",
        (idx, cols, tile_counts, in_vmem(near_halo), a_near, cot_near, ws, wn, wo, upd, xe, acc, g),
        [SM] * 3 + [VM] * 6 + [ANY] + [VM] * 3,
        (full, xe_t, acc_t, g_t, strip),
        (ANY,) + (VM,) * 4,
        [strip, acat_t, strip, da_t, pltpu.SemaphoreType.DMA],
        {9: 0, 10: 1, 11: 2, 12: 3},
    )
    near_recv = lax.ppermute(near_msg, "dom", near_pairs)
    xe, keep, send, act, d_pre, acat = call(
        far_kernel, "far_rows",
        (idx, cols, tile_counts, in_vmem(far_halo), a_far, cot_far, ws, wn, wo, xe, g),
        [SM] * 3 + [VM] * 8,
        (xe_t, half_t, half_t, strip, strip, acat_t),
        (VM,) * 6,
        [strip, g_t],
        {9: 0},
    )
    kept = {}

    def held(value, before):
        value, before = lax.optimization_barrier((value, before))
        return value, before

    def message(after, before):
        gate, _ = lax.optimization_barrier((idx, after))
        kept["acc"], msg = call(
            message_kernel, "messages",
            (gate, cols, d_pre, acat, wn, acc),
            [SM] * 2 + [VM] * 4,
            (acc_t, strip),
            (VM, VM),
            [da_t],
            {5: 0},
        )
        kept["msg"], before = held(msg, before)
        return before

    def send_far(name, sides):
        def hook(after, before):
            msg, _ = lax.optimization_barrier((kept["msg"], after))
            kept[name] = lax.ppermute(msg, "dom", [p for p in far_pairs if p[0] % 4 in sides])
            return before

        return hook

    def own(after, before):
        gate, _ = lax.optimization_barrier((idx, after))
        kept["upd"], grad, kept["edge"] = call(
            own_kernel, "own_rows",
            (gate, in_vmem(near_recv), act, d_pre, cot_far, xe, kept["acc"], ws, wo, upd),
            [SM] + [VM] * 8 + [ANY],
            (full, full, pltpu.VMEM((clones, width, hidden), F32)),
            (ANY, ANY, VM),
            [strip, pltpu.VMEM((clones, rows - width, hidden), BF16), pltpu.SemaphoreType.DMA((3,))],
            {9: 0},
        )
        kept["grad"], before = held(grad, before)
        return before

    def edge(after, before):
        gate, _ = lax.optimization_barrier((idx, after))
        grad = call(
            edge_kernel, "edge_rows",
            (gate, kept["edge"], in_vmem(kept["straight"]), in_vmem(kept["across"]), kept["grad"]),
            [SM, VM, VM, VM, ANY],
            full,
            ANY,
            [strip, pltpu.SemaphoreType.DMA],
            {4: 0},
        )
        kept["grad"], before = held(grad, before)
        return before

    factor = 1.0 / math.sqrt(2.0 * rows * count)
    hooks = {0: (message, send_far("across", (0, 3)),), 2: (send_far("straight", (1, 2)),)}
    for at, hook in ((OWN_AT, own), (EDGE_AT, edge)):
        hooks[at] = hooks.get(at, ()) + (hook,)
    sums = reduce_all(call, keep, send, idx, factor, hooks)
    return (
        kept["upd"],
        kept["grad"],
        *sums,
    )


def solution(mesh):
    return jax.shard_map(
        body,
        mesh=mesh,
        in_specs=(
            P("groups", "dom", None),
            P("groups", "dom", None),
            P("dom", None, None, None),
            P("dom", None),
            P("dom"),
            P(),
            P(),
            P(),
        ),
        out_specs=(
            P("groups", "dom", None),
            P("groups", "dom", None),
            P("groups", None),
            P("groups", None),
            P("groups", None),
        ),
        check_vma=False,
    )
```

```python
import functools
import math

import jax
import jax.numpy as jnp
from jax import lax
from jax.experimental import pallas as pl
from jax.experimental.pallas import tpu as pltpu
from jax.sharding import PartitionSpec as P

R = 4
F32 = jnp.float32
BF16 = jnp.bfloat16
ANY = pl.BlockSpec(memory_space=pltpu.HBM)
VM = pl.BlockSpec(memory_space=pltpu.VMEM)
SM = pl.BlockSpec(memory_space=pltpu.SMEM)
OWN_AT, EDGE_AT = 2, 3
COSTS = dict(mid_rows=1, near_rows=1, far_rows=1, messages=1, own_rows=1, edge_rows=1)
LIMIT = 12 * 1024 * 1024


def mm(a, b):
    return lax.dot_general(a, b, (((1,), (0,)), ((), ())), preferred_element_type=F32)


def mm_bt(a, b):
    return lax.dot_general(a, b, (((1,), (1,)), ((), ())), preferred_element_type=F32)


def mm_at(a, b):
    return lax.dot_general(a, b, (((0,), (0,)), ((), ())), preferred_element_type=F32)


def block_at(index, size):
    return pl.ds(pl.multiple_of(index * size, size), size)


def start_all(copies):
    for copy in copies:
        copy.start()
    return copies


def wait_all(copies):
    for copy in copies:
        copy.wait()


def in_vmem(value):
    return pltpu.with_memory_space_constraint(value, pltpu.VMEM)


def in_hbm(value):
    return pltpu.with_memory_space_constraint(value, pltpu.HBM)


def aggregate_rows(a_ref, acat_ref, agg_ref, x_ref, cols, live):
    slots, size = a_ref.shape[1:3]
    for r in range(R):
        acat = jnp.concatenate(
            [jnp.where(k < live(r), a_ref[r, k], jnp.zeros((), BF16)) for k in range(slots)], axis=1
        )
        acat_ref[r] = acat
        for c in range(x_ref.shape[0]):
            picked = jnp.concatenate(
                [x_ref[c, block_at(cols(r, k), size), :] for k in range(slots)], axis=0
            )
            agg_ref[c, r * size : (r + 1) * size, :] = mm(acat, picked).astype(BF16)


def dense_forward(x, agg, cot, ws, wn, wo):
    pre = mm(x, ws) + mm(agg, wn)
    sigma = jax.nn.sigmoid(pre)
    act = (pre * sigma).astype(BF16)
    d_pre = (mm_bt(cot, wo) * sigma * (1.0 + pre * (1.0 - sigma))).astype(BF16)
    return act, d_pre


def add_grads(g_ref, x, agg, act, cot, d_pre, fresh):
    hidden = d_pre.shape[1]
    for p, part in enumerate((mm_at(x, d_pre), mm_at(agg, d_pre), mm_at(act, cot))):
        sl = slice(p * hidden, (p + 1) * hidden)
        if fresh:
            g_ref[sl, :] = part
        else:
            g_ref[sl, :] += part


def send_rows(acc_ref, acat_ref, da_ref, cols, slots):
    clones, _, hidden = acc_ref.shape
    size = acat_ref.shape[1]
    for r in range(R):
        msg = mm_at(acat_ref[r], da_ref[r * size : (r + 1) * size, :])
        for k in range(slots):
            at = block_at(cols(r, k), size)
            for c in range(clones):
                acc_ref[c, at, :] += msg[k * size : (k + 1) * size, c * hidden : (c + 1) * hidden]


def whole_chunk(a_ref, cot_ref, xe, acc, g, upd_ref, acat_s, agg_s, da_s, ws, wn, wo, base, cols, live, fresh, late=()):
    clones, width, hidden = cot_ref.shape
    slots, size = a_ref.shape[1:3]
    rows = pl.ds(pl.multiple_of((base + R) * size, width), width)
    aggregate_rows(a_ref, acat_s, agg_s, xe, cols, live)
    wait_all(late)
    for c in range(clones):
        x, agg, cot = xe[c, rows, :], agg_s[c], cot_ref[c]
        act, d_pre = dense_forward(x, agg, cot, ws[...], wn[...], wo[...])
        upd_ref[c] = (x.astype(F32) + mm(act, wo[...])).astype(BF16)
        add_grads(g, x, agg, act, cot, d_pre, fresh and c == 0)
        da_s[:, c * hidden : (c + 1) * hidden] = mm_bt(d_pre, wn[...]).astype(BF16)
        acc[c, rows, :] += cot.astype(F32) + mm_bt(d_pre, ws[...])
    send_rows(acc, acat_s, da_s, cols, slots)


def mid_kernel(
    idx, cols_ref, cnt_ref, x_hbm, a_hbm, cot_hbm, ws_hbm, wn_hbm, wo_hbm,
    upd_hbm, xe, acc, g, a_near, a_far, cot_near, cot_far, ws, wn, wo,
    a_s, cot_s, upd_s, acat_s, agg_s, da_s, sems,
):
    clones, rows, hidden = x_hbm.shape
    per, slots, size, _ = a_hbm.shape
    width = R * size
    chunks = per // R - 2
    odd = lax.rem(idx[0], 2) == 1
    first = idx[0] * per - R
    near = jnp.where(odd, 0, per - R)
    far = jnp.where(odd, per - R, 0)
    count = iter(range(100))

    def load(source, target):
        copy = pltpu.make_async_copy(source, target, sems.at[next(count)])
        copy.start()
        return copy

    def rows_of(ref, row):
        return ref.at[:, pl.ds(pl.multiple_of(row * size, width), width), :]

    a_in, cot_in, x_in = [], [], []
    x_in.append([load(x_hbm.at[:, : 3 * width, :], xe.at[:, width : 4 * width, :])])
    for i in range(chunks):
        a_in.append(load(a_hbm.at[R + R * i : 2 * R + R * i], a_s.at[i]))
        cot_in.append(load(rows_of(cot_hbm, R + R * i), cot_s.at[i]))
        if i > 0:
            lo, hi = (i + 2) * width, (i + 3) * width
            x_in.append([load(x_hbm.at[:, lo:hi, :], xe.at[:, lo + width : hi + width, :])])
        if i == 0:
            weights = [load(*pair) for pair in ((ws_hbm, ws), (wn_hbm, wn), (wo_hbm, wo))]
    late = [
        load(a_hbm.at[pl.ds(near, R)], a_near),
        load(rows_of(cot_hbm, near), cot_near),
        load(a_hbm.at[pl.ds(far, R)], a_far),
        load(rows_of(cot_hbm, far), cot_far),
    ]
    acc[...] = jnp.zeros_like(acc)
    for i in range(chunks):
        base = R + R * i
        wait_all(x_in[i] + [a_in[i]])
        whole_chunk(
            a_s.at[i], cot_s.at[i], xe, acc, g, upd_s.at[i], acat_s, agg_s, da_s, ws, wn, wo, base,
            lambda r, k: cols_ref[k, base + r] - first, lambda r: cnt_ref[base + r], i == 0,
            [cot_in[i]] + (weights if i == 0 else []),
        )
        late.append(load(upd_s.at[i], rows_of(upd_hbm, base)))
    wait_all(late)


def near_kernel(
    idx, cols_ref, cnt_ref, halo, a_ref, cot_ref, ws, wn, wo, upd_in, xe_in, acc_in, g_in,
    upd_hbm, xe, acc, g, msg_ref,
    upd_s, acat_s, agg_s, da_s, sem,
):
    clones, width, hidden = halo.shape
    size = a_ref.shape[2]
    per = xe.shape[1] // size - 2 * R
    odd = lax.rem(idx[0], 2) == 1
    first = idx[0] * per - R
    base = jnp.where(odd, 0, per - R)
    outer = pl.ds(pl.multiple_of(jnp.where(odd, 0, R + per) * size, width), width)
    xe[:, outer, :] = halo[...]
    whole_chunk(
        a_ref, cot_ref, xe, acc, g, upd_s, acat_s, agg_s, da_s, ws, wn, wo, base,
        lambda r, k: cols_ref[k, base + r] - first, lambda r: cnt_ref[base + r], False,
    )
    store = pltpu.make_async_copy(
        upd_s, upd_hbm.at[:, pl.ds(pl.multiple_of(base * size, width), width), :], sem
    )
    store.start()
    msg_ref[...] = acc[:, outer, :].astype(BF16)
    store.wait()


def far_kernel(
    idx, cols_ref, cnt_ref, halo, a_ref, cot_ref, ws, wn, wo, xe_in, g_in,
    xe, keep_ref, send_ref, act_ref, dpre_ref, acat_ref,
    agg_s, g_s,
):
    clones, width, hidden = halo.shape
    size = a_ref.shape[2]
    per = xe.shape[1] // size - 2 * R
    odd = lax.rem(idx[0], 2)
    first = idx[0] * per - R
    base = jnp.where(odd == 1, per - R, 0)
    outer = pl.ds(pl.multiple_of(jnp.where(odd == 1, R + per, 0) * size, width), width)
    rows = pl.ds(pl.multiple_of((base + R) * size, width), width)
    xe[:, outer, :] = halo[...]
    aggregate_rows(
        a_ref, acat_ref, agg_s, xe,
        lambda r, k: cols_ref[k, base + r] - first, lambda r: cnt_ref[base + r],
    )
    g_s[...] = g_in[...]
    for c in range(clones):
        x, agg, cot = xe[c, rows, :], agg_s[c], cot_ref[c]
        act, d_pre = dense_forward(x, agg, cot, ws[...], wn[...], wo[...])
        act_ref[c] = act
        dpre_ref[c] = d_pre
        add_grads(g_s, x, agg, act, cot, d_pre, False)
    half = g_s.shape[0] // 2
    keep_ref[...] = g_s[pl.ds(pl.multiple_of(odd * half, half), half), :]
    send_ref[...] = g_s[pl.ds(pl.multiple_of((1 - odd) * half, half), half), :]


def message_kernel(idx, cols_ref, dpre, acat, wn, acc_in, acc, msg_ref, da_s):
    clones, width, hidden = dpre.shape
    size = acat.shape[1]
    per = acc.shape[1] // size - 2 * R
    odd = lax.rem(idx[0], 2) == 1
    first = idx[0] * per - R
    base = jnp.where(odd, per - R, 0)
    outer = pl.ds(pl.multiple_of(jnp.where(odd, R + per, 0) * size, width), width)
    for c in range(clones):
        da_s[:, c * hidden : (c + 1) * hidden] = mm_bt(dpre[c], wn[...]).astype(BF16)
    send_rows(acc, acat, da_s, lambda r, k: cols_ref[k, base + r] - first, acat.shape[2] // size)
    msg_ref[...] = acc[:, outer, :].astype(BF16)


def own_kernel(
    idx, nrecv, act, dpre, cot_ref, xe, acc, ws, wo, upd_in,
    upd_hbm, grad_hbm, edge_ref,
    upd_s, grad_s, sems,
):
    clones, width, hidden = act.shape
    rows = upd_hbm.shape[1]
    odd = lax.rem(idx[0], 2) == 1
    far = pl.multiple_of(jnp.where(odd, rows - width, 0), width)
    near = pl.multiple_of(jnp.where(odd, 0, rows - width), width)
    copies = []

    def store(source, target):
        copies.append(pltpu.make_async_copy(source, target, sems.at[len(copies)]))
        copies[-1].start()

    inner = rows - 2 * width
    grad_s[:, :inner, :] = acc[:, 2 * width : 2 * width + inner, :].astype(BF16)
    store(grad_s.at[:, pl.ds(0, inner), :], grad_hbm.at[:, pl.ds(width, inner), :])
    grad_s[:, inner:, :] = (
        acc[:, pl.ds(near + width, width), :] + nrecv[...].astype(F32)
    ).astype(BF16)
    store(grad_s.at[:, pl.ds(inner, width), :], grad_hbm.at[:, pl.ds(near, width), :])
    for c in range(clones):
        x = xe[c, pl.ds(far + width, width), :]
        upd_s[c] = (x.astype(F32) + mm(act[c], wo[...])).astype(BF16)
    store(upd_s, upd_hbm.at[:, pl.ds(far, width), :])
    for c in range(clones):
        edge_ref[c] = (
            acc[c, pl.ds(far + width, width), :] + cot_ref[c].astype(F32) + mm_bt(dpre[c], ws[...])
        )
    wait_all(copies)


def edge_kernel(idx, edge_ref, straight_ref, across_ref, grad_in, grad_hbm, out_s, sem):
    rows, width = grad_hbm.shape[1], edge_ref.shape[1]
    start = pl.multiple_of(jnp.where(lax.rem(idx[0], 2) == 1, rows - width, 0), width)
    received = straight_ref[...].astype(F32) + across_ref[...].astype(F32)
    out_s[...] = (edge_ref[...] + received).astype(BF16)
    out = pltpu.make_async_copy(out_s, grad_hbm.at[:, pl.ds(start, width), :], sem)
    out.start()
    out.wait()


def swap(value, bit):
    count = lax.axis_size("dom")
    return lax.ppermute(value, "dom", [(i, i ^ bit) for i in range(count)])


def half_rows(ref, bit):
    half = ref.shape[0] // 2
    return pl.ds(pl.multiple_of(bit * half, half), half)


def bit_of(idx, shift):
    return lax.rem(lax.shift_right_logical(idx[0], shift), 2)


def scatter_kernel(shift, idx, mine, other, keep_ref, send_ref):
    bit = bit_of(idx, shift)
    stay, leave = half_rows(mine, bit), half_rows(mine, 1 - bit)
    send_ref[...] = (mine[leave, :] + other[leave, :].astype(F32)).astype(BF16)
    keep_ref[...] = mine[stay, :] + other[stay, :].astype(F32)


def add_kernel(*refs):
    values = [ref[...].astype(F32) for ref in refs[:-1]]
    while len(values) > 1:
        values = [a + b for a, b in zip(values[::2], values[1::2])]
    refs[-1][...] = values[0].astype(BF16)


def join_kernel(shift, idx, mine, other, out_ref):
    bit = bit_of(idx, shift)
    out_ref[half_rows(out_ref, bit), :] = mine[...]
    out_ref[half_rows(out_ref, 1 - bit), :] = other[...]


def final_kernel(factor, idx, mine, other, gs_hbm, gn_hbm, go_hbm, all_s, out_s, sems):
    join_kernel(0, idx, mine, other, all_s)
    hidden = gs_hbm.shape[0]
    copies = []
    for p, ref in enumerate((gs_hbm, gn_hbm, go_hbm)):
        out_s[p] = all_s[p * hidden : (p + 1) * hidden, :].astype(F32) * factor
        copies.append(pltpu.make_async_copy(out_s.at[p], ref, sems.at[p]))
        copies[-1].start()
    wait_all(copies)


def reduce_all(call, keep, send, idx, factor, hooks):
    count = lax.axis_size("dom")
    hidden = keep.shape[1]
    stage = iter(range(100))
    sds = jax.ShapeDtypeStruct

    def vm(rows, kind):
        return pltpu.VMEM((rows, hidden), kind)

    def exchange(value, shift):
        moved = swap(value, 1 << shift)
        for hook in hooks.get(next(stage), ()):
            moved = hook(value, moved)
        return in_vmem(moved)

    mine, other = keep, exchange(send, 0)
    shifts = list(range(1, count.bit_length() - 1))
    scatter = shifts[1:2]
    for shift in scatter:
        rows = mine.shape[0] // 2
        mine, out = call(
            functools.partial(scatter_kernel, shift), "scatter", (idx, mine, other),
            [SM, VM, VM], (vm(rows, F32), vm(rows, BF16)), (VM, VM), [],
        )
        other = exchange(out, shift)
    mine = call(add_kernel, "add", (mine, other), [VM, VM], vm(mine.shape[0], BF16), VM, [])
    rest = [s for s in reversed(shifts) if s not in scatter]
    while rest:
        group, rest = rest[:2], rest[2:]
        masks = [1 << s for s in group]
        if len(masks) == 2:
            masks.append(masks[0] | masks[1])
        moved = [swap(mine, mask) for mask in masks]
        for hook in hooks.get(next(stage), ()):
            moved = hook(mine, moved)
        parts = (mine, *(in_vmem(part) for part in moved))
        mine = call(add_kernel, "add", parts, [VM] * len(parts), vm(mine.shape[0], BF16), VM, [])
    for shift in reversed(scatter):
        other = exchange(mine, shift)
        mine = call(
            functools.partial(join_kernel, shift), "join", (idx, mine, other),
            [SM, VM, VM], vm(2 * mine.shape[0], BF16), VM, [],
        )
    other = exchange(mine, 0)
    return call(
        functools.partial(final_kernel, factor), "final", (idx, mine, other),
        [SM, VM, VM], (sds((hidden, hidden), F32),) * 3, (ANY,) * 3,
        [vm(3 * hidden, BF16), pltpu.VMEM((3, hidden, hidden), F32), pltpu.SemaphoreType.DMA((3,))],
    )


def body(features, cotangent, adjacency, tile_cols, tile_counts, w_self, w_neigh, w_out):
    clones, rows, hidden = features.shape
    per, slots, size, _ = adjacency.shape
    width = R * size
    chunks = per // R - 2
    count = lax.axis_size("dom")
    index = lax.axis_index("dom")
    odd = (index & 1) == 1
    idx = index.reshape(1).astype(jnp.int32)
    cols = tile_cols.T
    near_pairs = [(i, i ^ 1) for i in range(count)]
    far_pairs = [(i, ((i + 1) ^ 1) - 1) for i in range(1, count - 1)]
    far_out = lax.dynamic_slice_in_dim(features, jnp.where(odd, rows - width, 0), width, axis=1)
    far_halo = lax.ppermute(far_out, "dom", far_pairs)
    near_out = lax.dynamic_slice_in_dim(features, jnp.where(odd, 0, rows - width), width, axis=1)
    near_halo = lax.ppermute(near_out, "dom", near_pairs)

    sds = jax.ShapeDtypeStruct
    full = sds((clones, rows, hidden), BF16)
    strip = pltpu.VMEM((clones, width, hidden), BF16)
    xe_t = pltpu.VMEM((clones, rows + 2 * width, hidden), BF16)
    acc_t = pltpu.VMEM((clones, rows + 2 * width, hidden), F32)
    g_t = pltpu.VMEM((3 * hidden, hidden), F32)
    half_t = pltpu.VMEM((3 * hidden // 2, hidden), F32)
    a_t = pltpu.VMEM((R, slots, size, size), BF16)
    acat_t = pltpu.VMEM((R, size, slots * size), BF16)
    da_t = pltpu.VMEM((width, clones * hidden), BF16)

    def call(kernel, name, ins, in_specs, outs, out_specs, scratch, aliases=None):
        return pl.pallas_call(
            kernel,
            out_shape=outs,
            in_specs=in_specs,
            out_specs=out_specs,
            scratch_shapes=scratch,
            input_output_aliases=aliases or {},
            compiler_params=pltpu.CompilerParams(vmem_limit_bytes=LIMIT),
            cost_estimate=pl.CostEstimate(flops=COSTS.get(name, 1), transcendentals=0, bytes_accessed=0),
            name=name,
        )(*ins)

    w_t = pltpu.VMEM((hidden, hidden), BF16)
    big = tuple(in_hbm(v) for v in (features, adjacency, cotangent, w_self, w_neigh, w_out))
    upd, xe, acc, g, a_near, a_far, cot_near, cot_far, ws, wn, wo = call(
        mid_kernel, "mid_rows",
        (idx, cols, tile_counts) + big,
        [SM] * 3 + [ANY] * 6,
        (full, xe_t, acc_t, g_t, a_t, a_t, strip, strip, w_t, w_t, w_t),
        (ANY,) + (VM,) * 10,
        [
            pltpu.VMEM((chunks, R, slots, size, size), BF16),
            pltpu.VMEM((chunks, clones, width, hidden), BF16),
            pltpu.VMEM((chunks, clones, width, hidden), BF16),
            acat_t, strip, da_t,
            pltpu.SemaphoreType.DMA((4 * chunks + 7,)),
        ],
    )
    upd, xe, acc, g, near_msg = call(
        near_kernel, "near_rows",
        (idx, cols, tile_counts, in_vmem(near_halo), a_near, cot_near, ws, wn, wo, upd, xe, acc, g),
        [SM] * 3 + [VM] * 6 + [ANY] + [VM] * 3,
        (full, xe_t, acc_t, g_t, strip),
        (ANY,) + (VM,) * 4,
        [strip, acat_t, strip, da_t, pltpu.SemaphoreType.DMA],
        {9: 0, 10: 1, 11: 2, 12: 3},
    )
    near_recv = lax.ppermute(near_msg, "dom", near_pairs)
    xe, keep, send, act, d_pre, acat = call(
        far_kernel, "far_rows",
        (idx, cols, tile_counts, in_vmem(far_halo), a_far, cot_far, ws, wn, wo, xe, g),
        [SM] * 3 + [VM] * 8,
        (xe_t, half_t, half_t, strip, strip, acat_t),
        (VM,) * 6,
        [strip, g_t],
        {9: 0},
    )
    kept = {}

    def held(value, before):
        value, before = lax.optimization_barrier((value, before))
        return value, before

    def message(after, before):
        gate, _ = lax.optimization_barrier((idx, after))
        kept["acc"], msg = call(
            message_kernel, "messages",
            (gate, cols, d_pre, acat, wn, acc),
            [SM] * 2 + [VM] * 4,
            (acc_t, strip),
            (VM, VM),
            [da_t],
            {5: 0},
        )
        kept["msg"], before = held(msg, before)
        return before

    def send_far(name, sides):
        def hook(after, before):
            msg, _ = lax.optimization_barrier((kept["msg"], after))
            kept[name] = lax.ppermute(msg, "dom", [p for p in far_pairs if p[0] % 4 in sides])
            return before

        return hook

    def own(after, before):
        gate, _ = lax.optimization_barrier((idx, after))
        kept["upd"], grad, kept["edge"] = call(
            own_kernel, "own_rows",
            (gate, in_vmem(near_recv), act, d_pre, cot_far, xe, kept["acc"], ws, wo, upd),
            [SM] + [VM] * 8 + [ANY],
            (full, full, pltpu.VMEM((clones, width, hidden), F32)),
            (ANY, ANY, VM),
            [strip, pltpu.VMEM((clones, rows - width, hidden), BF16), pltpu.SemaphoreType.DMA((3,))],
            {9: 0},
        )
        kept["grad"], before = held(grad, before)
        return before

    def edge(after, before):
        gate, _ = lax.optimization_barrier((idx, after))
        grad = call(
            edge_kernel, "edge_rows",
            (gate, kept["edge"], in_vmem(kept["straight"]), in_vmem(kept["across"]), kept["grad"]),
            [SM, VM, VM, VM, ANY],
            full,
            ANY,
            [strip, pltpu.SemaphoreType.DMA],
            {4: 0},
        )
        kept["grad"], before = held(grad, before)
        return before

    factor = 1.0 / math.sqrt(2.0 * rows * count)
    hooks = {0: (message, send_far("across", (0, 3))), 2: (send_far("straight", (1, 2)),)}
    for at, hook in ((OWN_AT, own), (EDGE_AT, edge)):
        hooks[at] = hooks.get(at, ()) + (hook,)
    sums = reduce_all(call, keep, send, idx, factor, hooks)
    return (
        kept["upd"],
        kept["grad"],
        *sums,
    )


def solution(mesh):
    return jax.shard_map(
        body,
        mesh=mesh,
        in_specs=(
            P("groups", "dom", None),
            P("groups", "dom", None),
            P("dom", None, None, None),
            P("dom", None),
            P("dom"),
            P(),
            P(),
            P(),
        ),
        out_specs=(
            P("groups", "dom", None),
            P("groups", "dom", None),
            P("groups", None),
            P("groups", None),
            P("groups", None),
        ),
        check_vma=False,
    )
```
